32 devices in a mesh: group: 4 (over y, core), span: 8 (over z, x).
Axes of the slice: x: 2, y: 2, z: 4, core: 2. Of those that a mesh axis runs over, the one named last changes fastest.
Arguments:
- tokens: bfloat16 [4096, 1024], P(('group', 'span')), may hold values from -32 to 32
- query_weight: bfloat16 [1024, 1024], replicated, may hold values from -0.1875 to 0.1875
- key_weight: bfloat16 [1024, 1024], replicated, may hold values from -0.1875 to 0.1875
- value_weight: bfloat16 [1024, 1024], replicated, may hold values from -0.1875 to 0.1875
- log_decay: float32 [16, 4096], P(None, ('group', 'span')), may hold values from -0.6 to 0
- neighbour_blocks: int32 [32, 4], P(('group', 'span')), may hold values from 0 to 31, as said below
- cotangent: bfloat16 [4096, 1024], P(('group', 'span')), may hold values from -6 to 6
Outputs:
- layer_out: bfloat16 [4096, 1024], P(('group', 'span'))
- tokens_grad: bfloat16 [4096, 1024], P(('group', 'span'))
- query_grad: bfloat16 [1024, 1024], replicated
- key_grad: bfloat16 [1024, 1024], replicated
- value_grad: bfloat16 [1024, 1024], replicated
The draws below stay inside these ranges and needn't reach their ends.
Inputs may be any that keep to these rules, and one draw needn't show every extreme that they name: `neighbour_blocks`: row b is [b, b - 1, b - 1, b - 1]; any entry that would fall before block 0 is block 0.
All inputs are finite; a program needn't handle non-finite values.
Results may differ from the reference program's by a relative error of at most 0.0077.
Values may be sent and summed in bfloat16 or wider, within the bound.
A program may use at most 192 MiB of HBM per device.

```python
import math
import jax
import jax.numpy as jnp
from jax import lax

D = 1024
ATTENDER_NUMBER = 16
DH = 64
TOK_DEV = 128
BLK = 128
NB = 4
FRAME_ELEMENTS = 4096


def draw_tokens(key, part):
    base_vals = jnp.clip(jax.random.normal(jax.random.fold_in(key, 1), (FRAME_ELEMENTS, D), jnp.float32), -4.5, 4.5)
    return base_vals.astype(jnp.bfloat16)


def attention_pair(key):
    first_matrix = jnp.clip(jax.random.normal(jax.random.fold_in(key, 11), (D, D), jnp.float32), -6.0, 6.0) / math.sqrt(D)
    other_matrix = jnp.clip(jax.random.normal(jax.random.fold_in(key, 12), (D, D), jnp.float32), -6.0, 6.0) / math.sqrt(D)
    second_matrix = other_matrix
    return (first_matrix, second_matrix)


def draw_query_weight(key, part):
    return attention_pair(key)[0].astype(jnp.bfloat16)


def draw_key_weight(key, part):
    return attention_pair(key)[1].astype(jnp.bfloat16)


def draw_log_decay(key, part):
    lookup_fragments = jax.random.split(key, 6)
    fast_share = 0.5
    seg_count = FRAME_ELEMENTS // TOK_DEV
    is_fast = jax.random.uniform(lookup_fragments[0], (ATTENDER_NUMBER, 1, 1), jnp.float32) < fast_share
    fast_rate = jnp.exp(jax.random.uniform(lookup_fragments[1], (ATTENDER_NUMBER, 1, 1), jnp.float32, math.log(1.0 / 50.0), math.log(1.0 / 30.0)))
    slow_rate = jnp.exp(jax.random.uniform(lookup_fragments[2], (ATTENDER_NUMBER, 1, 1), jnp.float32, math.log(0.1), math.log(0.4))) / FRAME_ELEMENTS
    device_factor = jnp.exp(jax.random.uniform(lookup_fragments[3], (ATTENDER_NUMBER, seg_count, 1), jnp.float32, math.log(0.5), math.log(2.0)))
    default_forget_factors = -jnp.broadcast_to(jnp.where(is_fast, fast_rate, slow_rate) * device_factor, (ATTENDER_NUMBER, seg_count, TOK_DEV)).reshape(ATTENDER_NUMBER, FRAME_ELEMENTS)
    pulse_volley_locations = jax.random.randint(lookup_fragments[4], (2,), 0, FRAME_ELEMENTS)
    pulse_volley_extent = jax.random.uniform(lookup_fragments[5], (ATTENDER_NUMBER, 2), jnp.float32, 0.22, 0.5)
    pairing_tallies = (jnp.arange(FRAME_ELEMENTS)[None, :, None] == pulse_volley_locations[None, None, :]).astype(jnp.float32)
    return default_forget_factors - jnp.sum(pairing_tallies * pulse_volley_extent[:, None, :], axis=2)


def draw_neighbour_blocks(key, part):
    block_total = FRAME_ELEMENTS // BLK
    per_dev = TOK_DEV // BLK
    own_block = jnp.arange(block_total, dtype=jnp.int32)[:, None]
    reach_back = jax.random.randint(key, (block_total, NB - 2), 1, per_dev + 1)
    far_block = jnp.maximum(own_block - per_dev, 0)
    near_block = jnp.maximum(own_block - reach_back, 0)
    return jnp.concatenate([own_block, far_block, near_block], axis=1).astype(jnp.int32)


def steps_of(stream_key, shape, cuts, least, largest):
    level, own = 1.0, jax.random.fold_in(stream_key, 6)
    for axis_at, shards_of in cuts:
        heights = jnp.exp(jax.random.uniform(jax.random.fold_in(own, axis_at), (shards_of,), jnp.float32, least / len(cuts), largest / len(cuts)))
        level = level * jnp.repeat(heights, shape[axis_at] // shards_of).reshape([-1 if axis == axis_at else 1 for axis in range(len(shape))])
    return level


def scatter_about(own_key, shape, width, most, pieces=(), kind=jnp.bfloat16):
    level = steps_of(own_key, shape, pieces, -0.22, 0.18) if pieces else 1.0
    drawn = jax.random.normal(own_key, shape, jnp.float32) * width * level
    return jnp.minimum(jnp.maximum(drawn, -most), most).astype(kind)


def setup_inputs(seed: int = 0) -> dict:
    arg_keys = jax.random.split(jax.random.key(seed), 8)
    tokens = draw_tokens(jax.random.fold_in(arg_keys[7], 71), 0)
    query_weight = draw_query_weight(jax.random.fold_in(arg_keys[7], 71), 0)
    key_weight = draw_key_weight(jax.random.fold_in(arg_keys[7], 71), 0)
    value_weight = scatter_about(arg_keys[3], (D, D), D ** -0.5, 0.1875)
    log_decay = draw_log_decay(jax.random.fold_in(arg_keys[7], 71), 0)
    neighbour_blocks = draw_neighbour_blocks(jax.random.fold_in(arg_keys[7], 71), 0)
    cotangent = scatter_about(arg_keys[6], (FRAME_ELEMENTS, D), 1.0, 6.0, ((0, 32),))
    return {"tokens": tokens, "query_weight": query_weight, "key_weight": key_weight, "value_weight": value_weight, "log_decay": log_decay, "neighbour_blocks": neighbour_blocks, "cotangent": cotangent}


def rounded(values):
    return lax.optimization_barrier(values.astype(jnp.bfloat16)).astype(jnp.float32)

def summarize(rate_seg, query, key, value, grad_out):
    row_count, feat_width = query.shape
    head_count = rate_seg.shape[0]
    head_size = feat_width // head_count
    lin_scale = 1.0 / (head_size * math.sqrt(row_count))
    running = jnp.cumsum(rate_seg, axis=1)
    seg_total = running[:, -1]
    fading = jnp.exp(seg_total[:, None] - running).T[:, :, None]
    growth = jnp.exp(running).T[:, :, None]
    q_heads = query.reshape(row_count, head_count, head_size).astype(jnp.float32)
    k_heads = key.reshape(row_count, head_count, head_size).astype(jnp.float32)
    v_heads = value.reshape(row_count, head_count, head_size).astype(jnp.float32)
    g_heads = grad_out.reshape(row_count, head_count, head_size).astype(jnp.float32)
    weighted = rounded(v_heads * fading)
    local_state = jnp.einsum('shd,she->hde', k_heads, weighted)
    scaled_grad = rounded(g_heads * growth)
    head_grad = lin_scale * jnp.einsum('thd,the->hde', q_heads, scaled_grad)
    return (seg_total, local_state, head_grad)

def segment_work(rate_seg, query, keyval, prev_keyval, grad_out, local_ids, state_in, later):
    row_count, feat_width = query.shape
    head_count = rate_seg.shape[0]
    head_size = feat_width // head_count
    blocks = row_count // BLK
    lin_scale = 1.0 / (head_size * math.sqrt(row_count))
    soft_scale = 1.0 / math.sqrt(head_size)
    running = jnp.cumsum(rate_seg, axis=1)
    seg_total = running[:, -1]
    growth = jnp.exp(running).T[:, :, None]
    fading = jnp.exp(seg_total[:, None] - running).T[:, :, None]
    places = jnp.arange(row_count, dtype=jnp.int32)
    is_lower = places[:, None] >= places[None, :]
    decay_mat = jnp.where(is_lower[None], jnp.exp(jnp.minimum(running[:, :, None] - running[:, None, :], 0.0)), 0.0)
    q_heads = query.reshape(row_count, head_count, head_size).astype(jnp.float32)
    k_heads = keyval[:, :feat_width].reshape(row_count, head_count, head_size).astype(jnp.float32)
    v_heads = keyval[:, feat_width:].reshape(row_count, head_count, head_size).astype(jnp.float32)
    g_heads = grad_out.reshape(row_count, head_count, head_size).astype(jnp.float32)
    intra_mat = rounded(jnp.einsum('thd,shd->hts', q_heads, k_heads) * decay_mat)
    state_bf = rounded(state_in)
    linear_out = jnp.einsum('hts,she->the', intra_mat, v_heads) + growth * jnp.einsum('thd,hde->the', q_heads, state_bf)
    extended = jnp.concatenate([prev_keyval, keyval], axis=0).reshape(2 * blocks, BLK, 2 * feat_width)
    picked = jnp.take(extended, local_ids, axis=0).reshape(blocks, NB * BLK, 2 * feat_width).astype(jnp.float32)
    near_key = picked[:, :, :feat_width].reshape(blocks, NB * BLK, head_count, head_size)
    near_val = picked[:, :, feat_width:].reshape(blocks, NB * BLK, head_count, head_size)
    q_blocks = q_heads.reshape(blocks, BLK, head_count, head_size)
    g_blocks = g_heads.reshape(blocks, BLK, head_count, head_size)
    logits = jnp.einsum('bthd,bshd->bhts', q_blocks, near_key) * soft_scale
    row_peak = lax.optimization_barrier(jnp.max(logits, axis=-1, keepdims=True))
    exp_terms = jnp.exp(logits - row_peak)
    soft_probs = exp_terms / lax.optimization_barrier(jnp.sum(exp_terms, axis=-1, keepdims=True))
    probs_bf = rounded(soft_probs)
    near_out = jnp.einsum('bhts,bshd->bthd', probs_bf, near_val).reshape(row_count, head_count, head_size)
    layer_out = (lin_scale * linear_out + near_out).reshape(row_count, feat_width).astype(jnp.bfloat16)
    prob_grad = jnp.einsum('bthd,bshd->bhts', g_blocks, near_val)
    inner_sum = lax.optimization_barrier(jnp.sum(soft_probs * prob_grad, axis=-1, keepdims=True))
    dlogit = rounded(soft_probs * (prob_grad - inner_sum) * soft_scale)
    dq_near = jnp.einsum('bhts,bshd->bthd', dlogit, near_key).reshape(row_count, head_count, head_size)
    dk_near = jnp.einsum('bhts,bthd->bshd', dlogit, q_blocks).reshape(blocks * NB, BLK, feat_width)
    dv_near = jnp.einsum('bhts,bthd->bshd', probs_bf, g_blocks).reshape(blocks * NB, BLK, feat_width)
    dpicked = jnp.concatenate([dk_near, dv_near], axis=-1)
    onehot = (local_ids.reshape(-1)[:, None] == jnp.arange(2 * blocks, dtype=jnp.int32)[None, :]).astype(jnp.float32)
    ext_grad = jnp.einsum('nm,ntc->mtc', onehot, dpicked, precision=lax.Precision.HIGHEST).reshape(2 * row_count, 2 * feat_width)
    back_mat = rounded(jnp.einsum('thd,shd->hts', g_heads, v_heads) * decay_mat)
    later_bf = rounded(later)
    dq_lin = lin_scale * (jnp.einsum('hts,shd->thd', back_mat, k_heads) + growth * jnp.einsum('the,hde->thd', g_heads, state_bf))
    dk_lin = lin_scale * jnp.einsum('hts,thd->shd', back_mat, q_heads) + fading * jnp.einsum('she,hde->shd', v_heads, later_bf)
    dv_lin = lin_scale * jnp.einsum('hts,the->she', intra_mat, g_heads) + fading * jnp.einsum('shd,hde->she', k_heads, later_bf)
    query_delta = (dq_lin + dq_near).reshape(row_count, feat_width).astype(jnp.bfloat16)
    lin_kv = jnp.concatenate([dk_lin.reshape(row_count, feat_width), dv_lin.reshape(row_count, feat_width)], axis=1)
    own_grad = (lin_kv + ext_grad[row_count:]).astype(jnp.bfloat16)
    prev_grad = ext_grad[:row_count].astype(jnp.bfloat16)
    return (layer_out, query_delta, own_grad, prev_grad)

def reference(tokens, query_weight, key_weight, value_weight, log_decay, neighbour_blocks, cotangent):
    query = jnp.dot(tokens, query_weight, preferred_element_type=jnp.float32).astype(jnp.bfloat16)
    key = jnp.dot(tokens, key_weight, preferred_element_type=jnp.float32).astype(jnp.bfloat16)
    value = jnp.dot(tokens, value_weight, preferred_element_type=jnp.float32).astype(jnp.bfloat16)
    keyval = jnp.concatenate([key, value], axis=1)
    seg_count = FRAME_ELEMENTS // TOK_DEV
    per_dev = TOK_DEV // BLK
    rate_segs = log_decay.reshape(ATTENDER_NUMBER, seg_count, TOK_DEV).transpose(1, 0, 2)
    q_segs = query.reshape(seg_count, TOK_DEV, D)
    k_segs = key.reshape(seg_count, TOK_DEV, D)
    v_segs = value.reshape(seg_count, TOK_DEV, D)
    kv_segs = keyval.reshape(seg_count, TOK_DEV, 2 * D)
    g_segs = cotangent.reshape(seg_count, TOK_DEV, D)

    def summary_entry(entry):
        return summarize(entry[0], entry[1], entry[2], entry[3], entry[4])
    totals, states, head_grads = lax.map(summary_entry, (rate_segs, q_segs, k_segs, v_segs, g_segs))

    def advance(running_state, entry):
        return (jnp.exp(entry[0])[:, None, None] * running_state + entry[1], running_state)
    zero_state = jnp.zeros((ATTENDER_NUMBER, DH, DH), jnp.float32)
    _, state_in = lax.scan(advance, zero_state, (totals, states))
    _, later = lax.scan(advance, zero_state, (totals, head_grads), reverse=True)
    padded = jnp.concatenate([jnp.zeros((TOK_DEV, 2 * D), jnp.bfloat16), keyval], axis=0)
    block_ids = neighbour_blocks.reshape(seg_count, per_dev, NB)

    def work_entry(entry):
        seg_index = entry[0]
        prev_keyval = lax.dynamic_slice_in_dim(padded, (seg_index * TOK_DEV).astype(jnp.int32), TOK_DEV, 0)
        local_ids = (entry[5] - (seg_index - 1) * per_dev).astype(jnp.int32)
        return segment_work(entry[1], entry[2], entry[3], prev_keyval, entry[4], local_ids, entry[6], entry[7])
    outs_seg, delta_seg, own_seg, prev_seg = lax.map(work_entry, (jnp.arange(seg_count, dtype=jnp.int32), rate_segs, q_segs, kv_segs, g_segs, block_ids, state_in, later))
    layer_out = outs_seg.reshape(FRAME_ELEMENTS, D)
    query_delta = delta_seg.reshape(FRAME_ELEMENTS, D)
    own_grad = own_seg.reshape(FRAME_ELEMENTS, 2 * D)
    next_grad = jnp.concatenate([prev_seg[1:], jnp.zeros_like(prev_seg[:1])], axis=0).reshape(FRAME_ELEMENTS, 2 * D)
    tokens_grad = jnp.dot(query_delta, query_weight.T, preferred_element_type=jnp.float32)
    tokens_grad = tokens_grad + jnp.dot(own_grad[:, :D], key_weight.T, preferred_element_type=jnp.float32)
    tokens_grad = tokens_grad + jnp.dot(own_grad[:, D:], value_weight.T, preferred_element_type=jnp.float32)
    tokens_grad = tokens_grad + jnp.dot(next_grad[:, :D], key_weight.T, preferred_element_type=jnp.float32)
    tokens_grad = tokens_grad + jnp.dot(next_grad[:, D:], value_weight.T, preferred_element_type=jnp.float32)
    grad_norm = 1.0 / math.sqrt(FRAME_ELEMENTS)
    query_grad = jnp.dot(tokens.T, query_delta, preferred_element_type=jnp.float32) * grad_norm
    key_grad = (jnp.dot(tokens.T, own_grad[:, :D], preferred_element_type=jnp.float32) + jnp.dot(tokens.T, next_grad[:, :D], preferred_element_type=jnp.float32)) * grad_norm
    value_grad = (jnp.dot(tokens.T, own_grad[:, D:], preferred_element_type=jnp.float32) + jnp.dot(tokens.T, next_grad[:, D:], preferred_element_type=jnp.float32)) * grad_norm
    return (layer_out, tokens_grad.astype(jnp.bfloat16), query_grad.astype(jnp.bfloat16), key_grad.astype(jnp.bfloat16), value_grad.astype(jnp.bfloat16))
```

```python
import functools
import math

import jax
import jax.numpy as jnp
from jax import lax
from jax.experimental import pallas as pl
from jax.experimental.pallas import tpu as pltpu
from jax.sharding import PartitionSpec as P

AXES = ("group", "span")
F32 = jnp.float32
BF16 = jnp.bfloat16
ROWS = (((0,), (0,)), ((), ()))
COLS = (((1,), (1,)), ((), ()))


def shifted(block, axis, distance):
    devices = range(lax.axis_size(axis))
    route = [(i - distance, i) for i in devices if i - distance in devices]
    return lax.ppermute(block, axis, route)


def dot(a, b, dims=(((1,), (0,)), ((), ()))):
    return lax.dot_general(a, b, dims, preferred_element_type=F32)


def summary_kernel(lin_scale, size, q, k, v, g, col, out):
    heads = q.shape[1] // size
    states, grads = [], []
    for j in range(heads):
        cut = slice(j * size, (j + 1) * size)
        run = col[0, :, j : j + 1]
        fading = jnp.exp(run[run.shape[0] - 1 :, :] - run)
        weighted = (v[:, cut].astype(F32) * fading).astype(BF16)
        scaled = (g[:, cut].astype(F32) * jnp.exp(run)).astype(BF16)
        states.append(dot(k[:, cut], weighted, ROWS))
        grads.append(lin_scale * dot(q[:, cut], scaled, ROWS))
    out[:size, :] = jnp.concatenate(states, axis=1).astype(BF16)
    out[size:, :] = jnp.concatenate(grads, axis=1).astype(BF16)


def near_kernel(
    lin_scale, soft_scale, size, q, k, v, g, pk, pv, col, row, count,
    out, dq, own_k, own_v, prev_k, prev_v,
):
    rows = q.shape[0]
    heads = q.shape[1] // size
    t = lax.broadcasted_iota(jnp.int32, (rows, rows), 0)
    s = lax.broadcasted_iota(jnp.int32, (rows, rows), 1)
    lower = t >= s
    times = count[...]
    outs, dqs, dkv, dvv = [], [], [], []
    for j in range(heads):
        cut = slice(j * size, (j + 1) * size)
        qh, gh = q[:, cut], g[:, cut]
        kh = jnp.concatenate([k[:, cut], pk[:, cut]], axis=0)
        vh = jnp.concatenate([v[:, cut], pv[:, cut]], axis=0)
        decay = jnp.where(
            lower, jnp.exp(jnp.minimum(col[0, :, j : j + 1] - row[0, j : j + 1, :], 0.0)), 0.0
        ) * lin_scale
        score = dot(qh, kh, COLS)
        grad = dot(gh, vh, COLS)
        logits = jnp.where(times > 0.0, score * soft_scale, -1e30)
        peak = jnp.max(logits, axis=1, keepdims=True)
        terms = jnp.exp(logits - peak) * times
        probs = terms / jnp.sum(terms, axis=1, keepdims=True)
        inner = jnp.sum(probs * grad, axis=1, keepdims=True)
        dlogit = probs * (grad - inner) * soft_scale
        mix = jnp.concatenate(
            [probs[:, :rows] + score[:, :rows] * decay, probs[:, rows:]], axis=1
        ).astype(BF16)
        dmix = jnp.concatenate(
            [dlogit[:, :rows] + grad[:, :rows] * decay, dlogit[:, rows:]], axis=1
        ).astype(BF16)
        outs.append(dot(mix, vh))
        dqs.append(dot(dmix, kh))
        dkv.append(dot(dmix, qh, ROWS))
        dvv.append(dot(mix, gh, ROWS))
    out[...] = jnp.concatenate(outs, axis=1)
    dq[...] = jnp.concatenate(dqs, axis=1)
    dk = jnp.concatenate(dkv, axis=1)
    dv = jnp.concatenate(dvv, axis=1)
    own_k[...] = dk[:rows]
    own_v[...] = dv[:rows]
    prev_k[...] = dk[rows:].astype(BF16)
    prev_v[...] = dv[rows:].astype(BF16)


def state_kernel(
    lin_scale, size, q, k, v, g, col, gathered, wf, wb, out, dq, own_k, own_v,
    layer, delta, grad_k, grad_v,
):
    heads = q.shape[1] // size
    count = gathered.shape[0]

    def one(f, carry):
        block = gathered[f].astype(F32)
        return (
            carry[0] + wf[pl.ds(f, 1), :] * block[:size],
            carry[1] + wb[pl.ds(f, 1), :] * block[size:],
        )

    zero = jnp.zeros((size, q.shape[1]), F32)
    state, later = lax.fori_loop(0, count, one, (zero, zero), unroll=8)
    state, later = state.astype(BF16), later.astype(BF16)
    outs, dqs, dks, dvs = [], [], [], []
    for j in range(heads):
        cut = slice(j * size, (j + 1) * size)
        run = col[0, :, j : j + 1]
        growth = lin_scale * jnp.exp(run)
        fading = jnp.exp(run[run.shape[0] - 1 :, :] - run)
        st, lt = state[:, cut], later[:, cut]
        outs.append(growth * dot(q[:, cut], st))
        dqs.append(growth * dot(g[:, cut], st, COLS))
        dks.append(fading * dot(v[:, cut], lt, COLS))
        dvs.append(fading * dot(k[:, cut], lt))
    layer[...] = (out[...] + jnp.concatenate(outs, axis=1)).astype(BF16)
    delta[...] = (dq[...] + jnp.concatenate(dqs, axis=1)).astype(BF16)
    grad_k[...] = (own_k[...] + jnp.concatenate(dks, axis=1)).astype(BF16)
    grad_v[...] = (own_v[...] + jnp.concatenate(dvs, axis=1)).astype(BF16)


def attention_parts(row_count, feat_width, head_count):
    size = feat_width // head_count
    pair = 128 // size
    steps = head_count // pair
    lanes = pair * size
    wide = pl.BlockSpec((row_count, lanes), lambda i: (0, i))
    col = pl.BlockSpec((1, row_count, pair), lambda i: (i, 0, 0))
    row = pl.BlockSpec((1, pair, row_count), lambda i: (i, 0, 0))
    return size, pair, steps, lanes, wide, col, row


def project(inputs, weight):
    return dot(inputs, weight).astype(BF16)


def shards(tokens, query_weight, key_weight, value_weight, log_decay, neighbour_blocks, cotangent):
    row_count, feat_width = tokens.shape
    head_count = log_decay.shape[0]
    size, pair, steps, lanes, wide, col_spec, row_spec = attention_parts(
        row_count, feat_width, head_count
    )
    lin_scale = 1.0 / (size * math.sqrt(row_count))
    soft_scale = 1.0 / math.sqrt(size)
    devices = lax.axis_size(AXES)
    position = lax.axis_index(AXES)
    shape = lambda dtype: jax.ShapeDtypeStruct((row_count, feat_width), dtype)

    prev_tokens = shifted(tokens, AXES, 1)
    running = jnp.cumsum(log_decay, axis=1)
    totals = lax.all_gather(running[:, -1], AXES)
    row = running.reshape(steps, pair, row_count)
    col = row.transpose(0, 2, 1)
    query = project(tokens, query_weight)
    key = project(tokens, key_weight)
    value = project(tokens, value_weight)

    summary = pl.pallas_call(
        functools.partial(summary_kernel, lin_scale, size),
        grid=(steps,),
        in_specs=[wide] * 4 + [col_spec],
        out_specs=pl.BlockSpec((2 * size, lanes), lambda i: (0, i)),
        out_shape=jax.ShapeDtypeStruct((2 * size, feat_width), BF16),
        cost_estimate=pl.CostEstimate(flops=10**8, bytes_accessed=10**6, transcendentals=0),
    )(query, key, value, cotangent, col)
    gathered = lax.all_gather(summary, AXES)

    prev_key = project(prev_tokens, key_weight)
    prev_value = project(prev_tokens, value_weight)
    own_times = jnp.sum(neighbour_blocks == position).astype(F32)
    prev_times = jnp.sum(neighbour_blocks == position - 1).astype(F32)
    times = jnp.where(jnp.arange(2 * row_count) < row_count, own_times, prev_times)[None, :]
    out, dq, own_k, own_v, prev_gk, prev_gv = pl.pallas_call(
        functools.partial(near_kernel, lin_scale, soft_scale, size),
        grid=(steps,),
        in_specs=[wide] * 6 + [col_spec, row_spec, pl.BlockSpec((1, 2 * row_count), lambda i: (0, 0))],
        out_specs=[wide] * 6,
        out_shape=[shape(F32)] * 4 + [shape(BF16)] * 2,
        cost_estimate=pl.CostEstimate(flops=10**10, bytes_accessed=10**7, transcendentals=10**6),
    )(query, key, value, cotangent, prev_key, prev_value, col, row, times)

    owed = dot(prev_gk, key_weight, COLS) + dot(prev_gv, value_weight, COLS)
    owed = shifted(owed.astype(BF16), AXES, -1)

    places = jnp.arange(devices)
    ahead = places[None, :] > places[:, None]
    between = ahead & (places[None, :] < position)
    between_later = (places[None, :] < places[:, None]) & (places[None, :] > position)
    weigh = lambda mask: jnp.exp(jnp.sum(jnp.where(mask[:, :, None], totals[None], 0.0), axis=1))
    earlier = jnp.where(places[:, None] < position, weigh(between), 0.0)
    after = jnp.where(places[:, None] > position, weigh(between_later), 0.0)
    earlier = jnp.repeat(earlier, size, axis=1)
    after = jnp.repeat(after, size, axis=1)
    weight_spec = pl.BlockSpec((devices, lanes), lambda i: (0, i))
    layer_out, query_delta, grad_k, grad_v = pl.pallas_call(
        functools.partial(state_kernel, lin_scale, size),
        grid=(steps,),
        in_specs=[wide] * 4
        + [col_spec, pl.BlockSpec((devices, 2 * size, lanes), lambda i: (0, 0, i))]
        + [weight_spec] * 2
        + [wide] * 4,
        out_specs=[wide] * 4,
        out_shape=[shape(BF16)] * 4,
        cost_estimate=pl.CostEstimate(flops=10**9, bytes_accessed=10**7, transcendentals=0),
    )(query, key, value, cotangent, col, gathered, earlier, after, out, dq, own_k, own_v)

    grad_norm = 1.0 / math.sqrt(row_count * devices)
    query_part = dot(tokens, query_delta, ROWS)
    both = jnp.concatenate([tokens, prev_tokens], axis=0)
    key_part = dot(both, jnp.concatenate([grad_k, prev_gk], axis=0), ROWS)
    value_part = dot(both, jnp.concatenate([grad_v, prev_gv], axis=0), ROWS)
    grads = reduce_grads(
        [(part * grad_norm).astype(BF16) for part in (query_part, key_part, value_part)]
    )
    tokens_back = dot(query_delta, query_weight, COLS)
    tokens_back = tokens_back + dot(grad_k, key_weight, COLS) + dot(grad_v, value_weight, COLS)
    tokens_back = tokens_back + owed.astype(F32)
    return (layer_out, tokens_back.astype(BF16), *grads)


def reduce_grads(parts):
    return lax.psum(tuple(parts), AXES)


def solution(mesh):
    return jax.shard_map(
        shards,
        mesh=mesh,
        in_specs=(
            P(AXES, None),
            P(),
            P(),
            P(),
            P(None, AXES),
            P(AXES, None),
            P(AXES, None),
        ),
        out_specs=(P(AXES, None), P(AXES, None), P(), P(), P()),
        check_vma=False,
    )
```

```python
import functools
import math

import jax
import jax.numpy as jnp
from jax import lax
from jax.experimental import pallas as pl
from jax.experimental.pallas import tpu as pltpu
from jax.sharding import PartitionSpec as P

AXES = ("group", "span")
F32 = jnp.float32
BF16 = jnp.bfloat16
ROWS = (((0,), (0,)), ((), ()))
MESH = pl.DeviceIdType.MESH
COLS = (((1,), (1,)), ((), ()))


def shifted(block, axis, distance):
    devices = range(lax.axis_size(axis))
    route = [(i - distance, i) for i in devices if i - distance in devices]
    return lax.ppermute(block, axis, route)


def dot(a, b, dims=(((1,), (0,)), ((), ()))):
    return lax.dot_general(a, b, dims, preferred_element_type=F32)


def summary_kernel(lin_scale, size, q, k, v, g, col, out):
    heads = q.shape[1] // size
    states, grads = [], []
    for j in range(heads):
        cut = slice(j * size, (j + 1) * size)
        run = col[0, :, j : j + 1]
        fading = jnp.exp(run[run.shape[0] - 1 :, :] - run)
        weighted = (v[:, cut].astype(F32) * fading).astype(BF16)
        scaled = (g[:, cut].astype(F32) * jnp.exp(run)).astype(BF16)
        states.append(dot(k[:, cut], weighted, ROWS))
        grads.append(lin_scale * dot(q[:, cut], scaled, ROWS))
    out[:size, :] = jnp.concatenate(states, axis=1).astype(BF16)
    out[size:, :] = jnp.concatenate(grads, axis=1).astype(BF16)


def near_kernel(
    lin_scale, soft_scale, size, q, k, v, g, pk, pv, col, row, count,
    out, dq, own_k, own_v, prev_k, prev_v,
):
    rows = q.shape[0]
    heads = q.shape[1] // size
    t = lax.broadcasted_iota(jnp.int32, (rows, rows), 0)
    s = lax.broadcasted_iota(jnp.int32, (rows, rows), 1)
    lower = t >= s
    times = count[...]
    outs, dqs, dkv, dvv = [], [], [], []
    for j in range(heads):
        cut = slice(j * size, (j + 1) * size)
        qh, gh = q[:, cut], g[:, cut]
        kh = jnp.concatenate([k[:, cut], pk[:, cut]], axis=0)
        vh = jnp.concatenate([v[:, cut], pv[:, cut]], axis=0)
        decay = jnp.where(
            lower, jnp.exp(jnp.minimum(col[0, :, j : j + 1] - row[0, j : j + 1, :], 0.0)), 0.0
        ) * lin_scale
        score = dot(qh, kh, COLS)
        grad = dot(gh, vh, COLS)
        logits = jnp.where(times > 0.0, score * soft_scale, -1e30)
        peak = jnp.max(logits, axis=1, keepdims=True)
        terms = jnp.exp(logits - peak) * times
        probs = terms / jnp.sum(terms, axis=1, keepdims=True)
        inner = jnp.sum(probs * grad, axis=1, keepdims=True)
        dlogit = probs * (grad - inner) * soft_scale
        mix = jnp.concatenate(
            [probs[:, :rows] + score[:, :rows] * decay, probs[:, rows:]], axis=1
        ).astype(BF16)
        dmix = jnp.concatenate(
            [dlogit[:, :rows] + grad[:, :rows] * decay, dlogit[:, rows:]], axis=1
        ).astype(BF16)
        outs.append(dot(mix, vh))
        dqs.append(dot(dmix, kh))
        dkv.append(dot(dmix, qh, ROWS))
        dvv.append(dot(mix, gh, ROWS))
    out[...] = jnp.concatenate(outs, axis=1)
    dq[...] = jnp.concatenate(dqs, axis=1)
    dk = jnp.concatenate(dkv, axis=1)
    dv = jnp.concatenate(dvv, axis=1)
    own_k[...] = dk[:rows]
    own_v[...] = dv[:rows]
    prev_k[...] = dk[rows:].astype(BF16)
    prev_v[...] = dv[rows:].astype(BF16)


def state_kernel(
    lin_scale, size, q, k, v, g, col, carry, out, dq, own_k, own_v,
    layer, delta, grad_k, grad_v,
):
    heads = q.shape[1] // size
    state, later = carry[:size, :], carry[size:, :]
    outs, dqs, dks, dvs = [], [], [], []
    for j in range(heads):
        cut = slice(j * size, (j + 1) * size)
        run = col[0, :, j : j + 1]
        growth = lin_scale * jnp.exp(run)
        fading = jnp.exp(run[run.shape[0] - 1 :, :] - run)
        st, lt = state[:, cut], later[:, cut]
        outs.append(growth * dot(q[:, cut], st))
        dqs.append(growth * dot(g[:, cut], st, COLS))
        dks.append(fading * dot(v[:, cut], lt, COLS))
        dvs.append(fading * dot(k[:, cut], lt))
    layer[...] = (out[...] + jnp.concatenate(outs, axis=1)).astype(BF16)
    delta[...] = (dq[...] + jnp.concatenate(dqs, axis=1)).astype(BF16)
    grad_k[...] = (own_k[...] + jnp.concatenate(dks, axis=1)).astype(BF16)
    grad_v[...] = (own_v[...] + jnp.concatenate(dvs, axis=1)).astype(BF16)


def attention_parts(row_count, feat_width, head_count):
    size = feat_width // head_count
    pair = 128 // size
    steps = head_count // pair
    lanes = pair * size
    wide = pl.BlockSpec((row_count, lanes), lambda i: (0, i))
    col = pl.BlockSpec((1, row_count, pair), lambda i: (i, 0, 0))
    row = pl.BlockSpec((1, pair, row_count), lambda i: (i, 0, 0))
    return size, pair, steps, lanes, wide, col, row


def project(inputs, weight):
    return dot(inputs, weight).astype(BF16)


def shards(tokens, query_weight, key_weight, value_weight, log_decay, neighbour_blocks, cotangent):
    row_count, feat_width = tokens.shape
    head_count = log_decay.shape[0]
    size, pair, steps, lanes, wide, col_spec, row_spec = attention_parts(
        row_count, feat_width, head_count
    )
    lin_scale = 1.0 / (size * math.sqrt(row_count))
    soft_scale = 1.0 / math.sqrt(size)
    sizes = tuple(lax.axis_size(name) for name in AXES)
    devices = sizes[0] * sizes[1]
    position = lax.axis_index(AXES)
    shape = lambda dtype: jax.ShapeDtypeStruct((row_count, feat_width), dtype)

    prev_tokens = shifted(tokens, AXES, 1)
    running = jnp.cumsum(log_decay, axis=1)
    row = running.reshape(steps, pair, row_count)
    col = row.transpose(0, 2, 1)
    query = project(tokens, query_weight)
    key = project(tokens, key_weight)
    value = project(tokens, value_weight)

    summary = pl.pallas_call(
        functools.partial(summary_kernel, lin_scale, size),
        grid=(steps,),
        in_specs=[wide] * 4 + [col_spec],
        out_specs=pl.BlockSpec((2 * size, lanes), lambda i: (0, i)),
        out_shape=jax.ShapeDtypeStruct((2 * size, feat_width), BF16),
        cost_estimate=pl.CostEstimate(flops=10**8, bytes_accessed=10**6, transcendentals=0),
    )(query, key, value, cotangent, col)
    total = jnp.broadcast_to(jnp.repeat(running[:, -1], size)[None, :], (8, feat_width))
    carry = carried(summary, total, sizes)

    prev_key = project(prev_tokens, key_weight)
    prev_value = project(prev_tokens, value_weight)
    own_times = jnp.sum(neighbour_blocks == position).astype(F32)
    prev_times = jnp.sum(neighbour_blocks == position - 1).astype(F32)
    times = jnp.where(jnp.arange(2 * row_count) < row_count, own_times, prev_times)[None, :]
    out, dq, own_k, own_v, prev_gk, prev_gv = pl.pallas_call(
        functools.partial(near_kernel, lin_scale, soft_scale, size),
        grid=(steps,),
        in_specs=[wide] * 6 + [col_spec, row_spec, pl.BlockSpec((1, 2 * row_count), lambda i: (0, 0))],
        out_specs=[wide] * 6,
        out_shape=[shape(F32)] * 4 + [shape(BF16)] * 2,
        cost_estimate=pl.CostEstimate(flops=10**10, bytes_accessed=10**7, transcendentals=10**6),
    )(query, key, value, cotangent, prev_key, prev_value, col, row, times)

    owed = dot(prev_gk, key_weight, COLS) + dot(prev_gv, value_weight, COLS)
    owed = shifted(owed.astype(BF16), AXES, -1)

    layer_out, query_delta, grad_k, grad_v = pl.pallas_call(
        functools.partial(state_kernel, lin_scale, size),
        grid=(steps,),
        in_specs=[wide] * 4
        + [col_spec, pl.BlockSpec((2 * size, lanes), lambda i: (0, i))]
        + [wide] * 4,
        out_specs=[wide] * 4,
        out_shape=[shape(BF16)] * 4,
        cost_estimate=pl.CostEstimate(flops=10**9, bytes_accessed=10**7, transcendentals=0),
    )(query, key, value, cotangent, col, carry, out, dq, own_k, own_v)

    grad_norm = 1.0 / math.sqrt(row_count * devices)
    query_part = dot(tokens, query_delta, ROWS)
    both = jnp.concatenate([tokens, prev_tokens], axis=0)
    key_part = dot(both, jnp.concatenate([grad_k, prev_gk], axis=0), ROWS)
    value_part = dot(both, jnp.concatenate([grad_v, prev_gv], axis=0), ROWS)
    grads = reduce_grads(
        [(part * grad_norm).astype(BF16) for part in (query_part, key_part, value_part)],
        sizes,
    )
    tokens_back = dot(query_delta, query_weight, COLS)
    tokens_back = tokens_back + dot(grad_k, key_weight, COLS) + dot(grad_v, value_weight, COLS)
    tokens_back = tokens_back + owed.astype(F32)
    return (layer_out, tokens_back.astype(BF16), *grads)


def bits_of(axis, size):
    return [(axis, k) for k in range(size.bit_length() - 1)]


def bit_of(bit):
    return (lax.axis_index(bit[0]) // 2 ** bit[1]) % 2


def partner_of(bit):
    place = {name: lax.axis_index(name) for name in AXES}
    place[bit[0]] = place[bit[0]] + (1 - 2 * bit_of(bit)) * 2 ** bit[1]
    return place


def greet(bits):
    barrier = pltpu.get_barrier_semaphore()
    for bit in bits:
        pl.semaphore_signal(barrier, inc=1, device_id=partner_of(bit), device_id_type=MESH)
    pl.semaphore_wait(barrier, len(bits))


def carry_kernel(bits, size, x, total, out, sent, came, sums, sums_came, carry, sem, sum_sem):
    greet(bits)
    stages = len(bits)
    width = x.shape[1]
    tf = x[:size, :].astype(F32)
    tb = x[size:, :].astype(F32)
    carry[...] = jnp.zeros_like(carry)
    log_all = total[...]
    log_before = jnp.zeros_like(log_all)
    log_after = jnp.zeros_like(log_all)
    for i, bit in enumerate(bits):
        mine = bit_of(bit)
        if i:
            sums[i] = log_all
            sent[i, :size, :] = tf.astype(BF16)
            sent[i, size:, :] = tb.astype(BF16)
        copies = [
            pltpu.make_async_remote_copy(
                src_ref=sent.at[i] if i else x, dst_ref=came.at[i],
                send_sem=sem.at[0, i], recv_sem=sem.at[1, i],
                device_id=partner_of(bit), device_id_type=MESH,
            ),
            pltpu.make_async_remote_copy(
                src_ref=sums.at[i] if i else total, dst_ref=sums_came.at[i],
                send_sem=sum_sem.at[0, i], recv_sem=sum_sem.at[1, i],
                device_id=partner_of(bit), device_id_type=MESH,
            ),
        ]
        for copy in copies:
            copy.start()
        for copy in copies:
            copy.wait()
        log_other = sums_came[i]
        f_other = came[i, :size, :].astype(F32)
        b_other = came[i, size:, :].astype(F32)
        second = jnp.full((1, width), mine) == 1
        scale = jnp.exp(jnp.where(second, log_before, log_after)[:1])
        carry[:size, :] += jnp.where(second, scale, 0.0) * f_other
        carry[size:, :] += jnp.where(second, 0.0, scale) * b_other
        log_before = log_before + jnp.where(second, log_other, 0.0)
        log_after = log_after + jnp.where(second, 0.0, log_other)
        if i + 1 < stages:
            here, there = jnp.exp(log_all[:1]), jnp.exp(log_other[:1])
            one = jnp.ones_like(here)
            tf = jnp.where(second, one, there) * tf + jnp.where(second, here, one) * f_other
            tb = jnp.where(second, there, one) * tb + jnp.where(second, one, here) * b_other
            log_all = log_all + log_other
    out[...] = carry[...].astype(BF16)


def carried(summary, total, sizes):
    bits = bits_of("span", sizes[1]) + bits_of("group", sizes[0])
    rows, width = summary.shape
    stages = len(bits)
    vmem = pl.BlockSpec(memory_space=pltpu.VMEM)
    return pl.pallas_call(
        functools.partial(carry_kernel, bits, rows // 2),
        in_specs=[vmem, vmem],
        out_specs=vmem,
        out_shape=jax.ShapeDtypeStruct((rows, width), BF16),
        scratch_shapes=[
            pltpu.VMEM((stages, rows, width), BF16),
            pltpu.VMEM((stages, rows, width), BF16),
            pltpu.VMEM((stages, 8, width), F32),
            pltpu.VMEM((stages, 8, width), F32),
            pltpu.VMEM((rows, width), F32),
            pltpu.SemaphoreType.DMA((2, stages)),
            pltpu.SemaphoreType.DMA((2, stages)),
        ],
        compiler_params=pltpu.CompilerParams(collective_id=0, has_side_effects=True),
        cost_estimate=pl.CostEstimate(flops=10**9, bytes_accessed=10**8, transcendentals=0),
    )(summary, total)


def reduce_kernel(orders, *refs):
    count = len(orders)
    parts, outs = refs[:count], refs[count : 2 * count]
    held, acc, sem = refs[2 * count :]
    stages = len(orders[0])
    whole = parts[0].shape[0]
    greet(orders[0])
    low = [[0] for _ in orders]

    def halves(p, i):
        half = whole >> (i + 1)
        mine = bit_of(orders[p][i])
        keep = low[p][i] + mine * half
        give = low[p][i] + (1 - mine) * half
        return half, keep, give

    def copy(src, dst, p, i, slot):
        return pltpu.make_async_remote_copy(
            src_ref=src, dst_ref=dst, send_sem=sem.at[0, p, slot], recv_sem=sem.at[1, p, slot],
            device_id=partner_of(orders[p][i]), device_id_type=MESH,
        )

    def scatter(p, i):
        half, keep, give = halves(p, i)
        source = parts[p] if i == 0 else acc.at[p]
        place = whole - 2 * half
        return copy(source.at[pl.ds(give, half)], held.at[p, pl.ds(place, half)], p, i, i)

    def gather(p, i):
        half, keep, _ = halves(p, i)
        block = outs[p].at[pl.ds(keep, half)]
        return copy(block, block, p, i, stages + i)

    going = []
    for p in range(count):
        going.append(scatter(p, 0))
        going[p].start()
    for i in range(stages):
        for p in range(count):
            going[p].wait()
            half, keep, _ = halves(p, i)
            source = parts[p] if i == 0 else acc.at[p]
            target = acc.at[p] if i + 1 < stages else outs[p]
            place = whole - 2 * half
            step = min(half, 8)

            def add(c, _):
                at = pl.ds(keep + c * step, step)
                target[at] = source[at] + held[p, pl.ds(place + c * step, step)]
                return 0

            lax.fori_loop(0, half // step, add, 0)
            low[p].append(keep)
            going[p] = scatter(p, i + 1) if i + 1 < stages else gather(p, i)
            going[p].start()
    for i in reversed(range(stages)):
        for p in range(count):
            going[p].wait()
            if i:
                going[p] = gather(p, i - 1)
                going[p].start()


def reduce_grads(parts, sizes):
    group, span = bits_of("group", sizes[0]), bits_of("span", sizes[1])
    rest = group[1:] + span
    turns = [rest[k:3] + rest[:k] + rest[3:] for k in range(3)]
    orders = [group[:1] + turn for turn in turns]
    rows, width = parts[0].shape
    deep = (rows // 8, 8, width)
    vmem = pl.BlockSpec(memory_space=pltpu.VMEM)
    stages = len(orders[0])
    outs = pl.pallas_call(
        functools.partial(reduce_kernel, orders),
        in_specs=[vmem] * 3,
        out_specs=[vmem] * 3,
        out_shape=[jax.ShapeDtypeStruct(deep, BF16)] * 3,
        scratch_shapes=[
            pltpu.VMEM((3, *deep), BF16),
            pltpu.VMEM((3, *deep), BF16),
            pltpu.SemaphoreType.DMA((2, 3, 2 * stages)),
        ],
        compiler_params=pltpu.CompilerParams(
            collective_id=1, has_side_effects=True, vmem_limit_bytes=40 * 2**20
        ),
        cost_estimate=pl.CostEstimate(flops=10**9, bytes_accessed=10**8, transcendentals=0),
    )(*[part.reshape(deep) for part in parts])
    return [out.reshape(rows, width) for out in outs]


def solution(mesh):
    return jax.shard_map(
        shards,
        mesh=mesh,
        in_specs=(
            P(AXES, None),
            P(),
            P(),
            P(),
            P(None, AXES),
            P(AXES, None),
            P(AXES, None),
        ),
        out_specs=(P(AXES, None), P(AXES, None), P(), P(), P()),
        check_vma=False,
    )
```

```python
import functools
import math

import jax
import jax.numpy as jnp
from jax import lax
from jax.experimental import pallas as pl
from jax.experimental.pallas import tpu as pltpu
from jax.sharding import PartitionSpec as P

AXES = ("group", "span")
F32 = jnp.float32
BF16 = jnp.bfloat16
ROWS = (((0,), (0,)), ((), ()))
MESH = pl.DeviceIdType.MESH
COLS = (((1,), (1,)), ((), ()))


def shifted(block, axis, distance):
    devices = range(lax.axis_size(axis))
    route = [(i - distance, i) for i in devices if i - distance in devices]
    return lax.ppermute(block, axis, route)


def dot(a, b, dims=(((1,), (0,)), ((), ()))):
    return lax.dot_general(a, b, dims, preferred_element_type=F32)


def summary_kernel(lin_scale, size, q, k, v, g, col, out):
    heads = q.shape[1] // size
    states, grads = [], []
    for j in range(heads):
        cut = slice(j * size, (j + 1) * size)
        run = col[0, :, j : j + 1]
        fading = jnp.exp(run[run.shape[0] - 1 :, :] - run)
        weighted = (v[:, cut].astype(F32) * fading).astype(BF16)
        scaled = (g[:, cut].astype(F32) * jnp.exp(run)).astype(BF16)
        states.append(dot(k[:, cut], weighted, ROWS))
        grads.append(lin_scale * dot(q[:, cut], scaled, ROWS))
    out[:size, :] = jnp.concatenate(states, axis=1).astype(BF16)
    out[size:, :] = jnp.concatenate(grads, axis=1).astype(BF16)


def near_pair(lin_scale, soft_scale, size, q, k, v, g, pk, pv, col, row, times):
    rows = q.shape[0]
    heads = q.shape[1] // size
    t = lax.broadcasted_iota(jnp.int32, (rows, rows), 0)
    s = lax.broadcasted_iota(jnp.int32, (rows, rows), 1)
    lower = t >= s
    outs, dqs, dkv, dvv = [], [], [], []
    for j in range(heads):
        cut = slice(j * size, (j + 1) * size)
        qh, gh = q[:, cut], g[:, cut]
        kh = jnp.concatenate([k[:, cut], pk[:, cut]], axis=0)
        vh = jnp.concatenate([v[:, cut], pv[:, cut]], axis=0)
        decay = jnp.where(
            lower, jnp.exp(jnp.minimum(col[:, j : j + 1] - row[j : j + 1, :], 0.0)), 0.0
        ) * lin_scale
        score = dot(qh, kh, COLS)
        grad = dot(gh, vh, COLS)
        logits = jnp.where(times > 0.0, score * soft_scale, -1e30)
        peak = jnp.max(logits, axis=1, keepdims=True)
        terms = jnp.exp(logits - peak) * times
        probs = terms / jnp.sum(terms, axis=1, keepdims=True)
        inner = jnp.sum(probs * grad, axis=1, keepdims=True)
        dlogit = probs * (grad - inner) * soft_scale
        mix = jnp.concatenate(
            [probs[:, :rows] + score[:, :rows] * decay, probs[:, rows:]], axis=1
        ).astype(BF16)
        dmix = jnp.concatenate(
            [dlogit[:, :rows] + grad[:, :rows] * decay, dlogit[:, rows:]], axis=1
        ).astype(BF16)
        outs.append(dot(mix, vh))
        dqs.append(dot(dmix, kh))
        dkv.append(dot(dmix, qh, ROWS))
        dvv.append(dot(mix, gh, ROWS))
    dk = jnp.concatenate(dkv, axis=1)
    dv = jnp.concatenate(dvv, axis=1)
    return (
        jnp.concatenate(outs, axis=1),
        jnp.concatenate(dqs, axis=1),
        dk[:rows],
        dv[:rows],
        dk[rows:].astype(BF16),
        dv[rows:].astype(BF16),
    )


def state_kernel(
    lin_scale, size, q, k, v, g, col, carry, out, dq, own_k, own_v,
    layer, delta, grad_k, grad_v,
):
    heads = q.shape[1] // size
    state, later = carry[:size, :], carry[size:, :]
    outs, dqs, dks, dvs = [], [], [], []
    for j in range(heads):
        cut = slice(j * size, (j + 1) * size)
        run = col[0, :, j : j + 1]
        growth = lin_scale * jnp.exp(run)
        fading = jnp.exp(run[run.shape[0] - 1 :, :] - run)
        st, lt = state[:, cut], later[:, cut]
        outs.append(growth * dot(q[:, cut], st))
        dqs.append(growth * dot(g[:, cut], st, COLS))
        dks.append(fading * dot(v[:, cut], lt, COLS))
        dvs.append(fading * dot(k[:, cut], lt))
    layer[...] = (out[...] + jnp.concatenate(outs, axis=1)).astype(BF16)
    delta[...] = (dq[...] + jnp.concatenate(dqs, axis=1)).astype(BF16)
    grad_k[...] = (own_k[...] + jnp.concatenate(dks, axis=1)).astype(BF16)
    grad_v[...] = (own_v[...] + jnp.concatenate(dvs, axis=1)).astype(BF16)


def attention_parts(row_count, feat_width, head_count):
    size = feat_width // head_count
    pair = 128 // size
    steps = head_count // pair
    lanes = pair * size
    wide = pl.BlockSpec((row_count, lanes), lambda i: (0, i))
    col = pl.BlockSpec((1, row_count, pair), lambda i: (i, 0, 0))
    row = pl.BlockSpec((1, pair, row_count), lambda i: (i, 0, 0))
    return size, pair, steps, lanes, wide, col, row


def project(inputs, weight):
    return dot(inputs, weight).astype(BF16)


def shards(tokens, query_weight, key_weight, value_weight, log_decay, neighbour_blocks, cotangent):
    row_count, feat_width = tokens.shape
    head_count = log_decay.shape[0]
    size, pair, steps, lanes, wide, col_spec, row_spec = attention_parts(
        row_count, feat_width, head_count
    )
    lin_scale = 1.0 / (size * math.sqrt(row_count))
    soft_scale = 1.0 / math.sqrt(size)
    sizes = tuple(lax.axis_size(name) for name in AXES)
    devices = sizes[0] * sizes[1]
    position = lax.axis_index(AXES)
    shape = lambda dtype: jax.ShapeDtypeStruct((row_count, feat_width), dtype)

    prev_tokens = shifted(tokens, AXES, 1)
    running = jnp.cumsum(log_decay, axis=1)
    row = running.reshape(steps, pair, row_count)
    col = row.transpose(0, 2, 1)
    query = project(tokens, query_weight)
    key = project(tokens, key_weight)
    value = project(tokens, value_weight)

    summary = pl.pallas_call(
        functools.partial(summary_kernel, lin_scale, size),
        grid=(steps,),
        in_specs=[wide] * 4 + [col_spec],
        out_specs=pl.BlockSpec((2 * size, lanes), lambda i: (0, i)),
        out_shape=jax.ShapeDtypeStruct((2 * size, feat_width), BF16),
        cost_estimate=pl.CostEstimate(flops=10**8, bytes_accessed=10**6, transcendentals=0),
    )(query, key, value, cotangent, col)
    total = jnp.broadcast_to(jnp.repeat(running[:, -1], size)[None, :], (8, feat_width))

    prev_key = project(prev_tokens, key_weight)
    prev_value = project(prev_tokens, value_weight)
    own_times = jnp.sum(neighbour_blocks == position).astype(F32)
    prev_times = jnp.sum(neighbour_blocks == position - 1).astype(F32)
    times = jnp.where(jnp.arange(2 * row_count) < row_count, own_times, prev_times)[None, :]
    near = functools.partial(near_pair, lin_scale, soft_scale, size)
    operands = (query, key, value, cotangent, prev_key, prev_value, col, row, times)
    carry, out, dq, own_k, own_v, prev_gk, prev_gv = carried(near, summary, total, operands, sizes)

    owed = dot(prev_gk, key_weight, COLS) + dot(prev_gv, value_weight, COLS)
    owed = shifted(owed.astype(BF16), AXES, -1)

    layer_out, query_delta, grad_k, grad_v = pl.pallas_call(
        functools.partial(state_kernel, lin_scale, size),
        grid=(steps,),
        in_specs=[wide] * 4
        + [col_spec, pl.BlockSpec((2 * size, lanes), lambda i: (0, i))]
        + [wide] * 4,
        out_specs=[wide] * 4,
        out_shape=[shape(BF16)] * 4,
        cost_estimate=pl.CostEstimate(flops=10**9, bytes_accessed=10**7, transcendentals=0),
    )(query, key, value, cotangent, col, carry, out, dq, own_k, own_v)

    grad_norm = 1.0 / math.sqrt(row_count * devices)
    grads = reduce_grads(
        grad_norm,
        (tokens, prev_tokens, query_delta, grad_k, grad_v, prev_gk, prev_gv),
        sizes,
    )
    tokens_back = dot(query_delta, query_weight, COLS)
    tokens_back = tokens_back + dot(grad_k, key_weight, COLS) + dot(grad_v, value_weight, COLS)
    tokens_back = tokens_back + owed.astype(F32)
    return (layer_out, tokens_back.astype(BF16), *grads)


def bits_of(axis, size):
    return [(axis, k) for k in range(size.bit_length() - 1)]


def bit_of(bit):
    return (lax.axis_index(bit[0]) // 2 ** bit[1]) % 2


def partner_of(bit):
    place = {name: lax.axis_index(name) for name in AXES}
    place[bit[0]] = place[bit[0]] + (1 - 2 * bit_of(bit)) * 2 ** bit[1]
    return place


def greet(bits):
    barrier = pltpu.get_barrier_semaphore()
    for bit in bits:
        pl.semaphore_signal(barrier, inc=1, device_id=partner_of(bit), device_id_type=MESH)
    pl.semaphore_wait(barrier, len(bits))


def carry_kernel(bits, near, size, x, total, *refs):
    ins, col, row, count = refs[:6], refs[6], refs[7], refs[8]
    out, results = refs[9], refs[10:16]
    sent, came, sums, sums_came, carry, sem, sum_sem = refs[16:]
    steps, _, pair = col.shape
    lanes = pair * size

    def near_step(i, _):
        cut = pl.ds(pl.multiple_of(i * lanes, lanes), lanes)
        values = near(*(ref[:, cut] for ref in ins), col[i], row[i], count[...])
        for ref, value in zip(results, values):
            ref[:, cut] = value
        return 0

    greet(bits)
    stages = len(bits)
    width = x.shape[1]
    tf = x[:size, :].astype(F32)
    tb = x[size:, :].astype(F32)
    carry[...] = jnp.zeros_like(carry)
    log_all = total[...]
    log_before = jnp.zeros_like(log_all)
    log_after = jnp.zeros_like(log_all)
    for i, bit in enumerate(bits):
        mine = bit_of(bit)
        if i:
            sums[i] = log_all
            sent[i, :size, :] = tf.astype(BF16)
            sent[i, size:, :] = tb.astype(BF16)
        copies = [
            pltpu.make_async_remote_copy(
                src_ref=sent.at[i] if i else x, dst_ref=came.at[i],
                send_sem=sem.at[0, i], recv_sem=sem.at[1, i],
                device_id=partner_of(bit), device_id_type=MESH,
            ),
            pltpu.make_async_remote_copy(
                src_ref=sums.at[i] if i else total, dst_ref=sums_came.at[i],
                send_sem=sum_sem.at[0, i], recv_sem=sum_sem.at[1, i],
                device_id=partner_of(bit), device_id_type=MESH,
            ),
        ]
        for copy in copies:
            copy.start()
        lax.fori_loop(steps * i // stages, steps * (i + 1) // stages, near_step, 0)
        for copy in copies:
            copy.wait()
        log_other = sums_came[i]
        f_other = came[i, :size, :].astype(F32)
        b_other = came[i, size:, :].astype(F32)
        second = jnp.full((1, width), mine) == 1
        scale = jnp.exp(jnp.where(second, log_before, log_after)[:1])
        carry[:size, :] += jnp.where(second, scale, 0.0) * f_other
        carry[size:, :] += jnp.where(second, 0.0, scale) * b_other
        log_before = log_before + jnp.where(second, log_other, 0.0)
        log_after = log_after + jnp.where(second, 0.0, log_other)
        if i + 1 < stages:
            here, there = jnp.exp(log_all[:1]), jnp.exp(log_other[:1])
            one = jnp.ones_like(here)
            tf = jnp.where(second, one, there) * tf + jnp.where(second, here, one) * f_other
            tb = jnp.where(second, there, one) * tb + jnp.where(second, one, here) * b_other
            log_all = log_all + log_other
    out[...] = carry[...].astype(BF16)


def carried(near, summary, total, operands, sizes):
    bits = bits_of("span", sizes[1]) + bits_of("group", sizes[0])
    rows, width = summary.shape
    stages = len(bits)
    vmem = pl.BlockSpec(memory_space=pltpu.VMEM)
    return pl.pallas_call(
        functools.partial(carry_kernel, bits, near, rows // 2),
        in_specs=[vmem] * (2 + len(operands)),
        out_specs=[vmem] * 7,
        out_shape=[jax.ShapeDtypeStruct((rows, width), BF16)]
        + [jax.ShapeDtypeStruct(operands[0].shape, F32)] * 4
        + [jax.ShapeDtypeStruct(operands[0].shape, BF16)] * 2,
        scratch_shapes=[
            pltpu.VMEM((stages, rows, width), BF16),
            pltpu.VMEM((stages, rows, width), BF16),
            pltpu.VMEM((stages, 8, width), F32),
            pltpu.VMEM((stages, 8, width), F32),
            pltpu.VMEM((rows, width), F32),
            pltpu.SemaphoreType.DMA((2, stages)),
            pltpu.SemaphoreType.DMA((2, stages)),
        ],
        compiler_params=pltpu.CompilerParams(collective_id=0, has_side_effects=True),
        cost_estimate=pl.CostEstimate(flops=10**9, bytes_accessed=10**8, transcendentals=0),
    )(summary, total, *operands)


def reduce_kernel(orders, norm, tokens, prev, dq, dk, dv, pk, pv, *refs):
    count = len(orders)
    outs = refs[:count]
    made, held, acc, sem = refs[count:]
    parts = [made.at[p] for p in range(count)]
    deltas = ((dq, None), (dk, pk), (dv, pv))
    stages = len(orders[0])
    whole = outs[0].shape[0]
    greet(orders[0])

    def make(p, start):
        own, other = deltas[p]
        right = own[...] if other is None else jnp.concatenate([own[...], other[...]], axis=0)

        def one(c, _):
            cut = pl.ds(pl.multiple_of(start * 8 + c * 128, 128), 128)
            left = tokens[:, cut]
            if other is not None:
                left = jnp.concatenate([left, prev[:, cut]], axis=0)
            block = dot(left, right, ROWS) * norm
            made[p, pl.ds(start + c * 16, 16)] = block.reshape(16, 8, -1).astype(BF16)
            return 0

        lax.fori_loop(0, whole // 32, one, 0)

    low = [[0] for _ in orders]

    def halves(p, i):
        half = whole >> (i + 1)
        mine = bit_of(orders[p][i])
        keep = low[p][i] + mine * half
        give = low[p][i] + (1 - mine) * half
        return half, keep, give

    def copy(src, dst, p, i, slot):
        return pltpu.make_async_remote_copy(
            src_ref=src, dst_ref=dst, send_sem=sem.at[0, p, slot], recv_sem=sem.at[1, p, slot],
            device_id=partner_of(orders[p][i]), device_id_type=MESH,
        )

    def scatter(p, i):
        half, keep, give = halves(p, i)
        source = parts[p] if i == 0 else acc.at[p]
        place = whole - 2 * half
        return copy(source.at[pl.ds(give, half)], held.at[p, pl.ds(place, half)], p, i, i)

    def gather(p, i):
        half, keep, _ = halves(p, i)
        block = outs[p].at[pl.ds(keep, half)]
        return copy(block, block, p, i, stages + i)

    going = []
    for p in range(count):
        make(p, halves(p, 0)[2])
        going.append(scatter(p, 0))
        going[p].start()
    for p in range(count):
        make(p, halves(p, 0)[1])
    for i in range(stages):
        for p in range(count):
            going[p].wait()
            half, keep, _ = halves(p, i)
            source = parts[p] if i == 0 else acc.at[p]
            target = acc.at[p] if i + 1 < stages else outs[p]
            place = whole - 2 * half
            step = min(half, 8)

            def add(c, _):
                at = pl.ds(keep + c * step, step)
                target[at] = source[at] + held[p, pl.ds(place + c * step, step)]
                return 0

            lax.fori_loop(0, half // step, add, 0)
            low[p].append(keep)
            going[p] = scatter(p, i + 1) if i + 1 < stages else gather(p, i)
            going[p].start()
    for i in reversed(range(stages)):
        for p in range(count):
            going[p].wait()
            if i:
                going[p] = gather(p, i - 1)
                going[p].start()


def reduce_grads(norm, operands, sizes):
    group, span = bits_of("group", sizes[0]), bits_of("span", sizes[1])
    rest = group[1:] + span
    turns = [rest[k:3] + rest[:k] + rest[3:] for k in range(3)]
    orders = [group[:1] + turn for turn in turns]
    rows = width = operands[0].shape[1]
    deep = (rows // 8, 8, width)
    vmem = pl.BlockSpec(memory_space=pltpu.VMEM)
    stages = len(orders[0])
    outs = pl.pallas_call(
        functools.partial(reduce_kernel, orders, norm),
        in_specs=[vmem] * len(operands),
        out_specs=[vmem] * 3,
        out_shape=[jax.ShapeDtypeStruct(deep, BF16)] * 3,
        scratch_shapes=[
            pltpu.VMEM((3, *deep), BF16),
            pltpu.VMEM((3, *deep), BF16),
            pltpu.VMEM((3, *deep), BF16),
            pltpu.SemaphoreType.DMA((2, 3, 2 * stages)),
        ],
        compiler_params=pltpu.CompilerParams(
            collective_id=1, has_side_effects=True, vmem_limit_bytes=40 * 2**20
        ),
        cost_estimate=pl.CostEstimate(flops=10**9, bytes_accessed=10**8, transcendentals=0),
    )(*operands)
    return [out.reshape(rows, width) for out in outs]


def solution(mesh):
    return jax.shard_map(
        shards,
        mesh=mesh,
        in_specs=(
            P(AXES, None),
            P(),
            P(),
            P(),
            P(None, AXES),
            P(AXES, None),
            P(AXES, None),
        ),
        out_specs=(P(AXES, None), P(AXES, None), P(), P(), P()),
        check_vma=False,
    )
```

```python
import functools
import math

import jax
import jax.numpy as jnp
from jax import lax
from jax.experimental import pallas as pl
from jax.experimental.pallas import tpu as pltpu
from jax.sharding import PartitionSpec as P

AXES = ("group", "span")
F32 = jnp.float32
BF16 = jnp.bfloat16
ROWS = (((0,), (0,)), ((), ()))
MESH = pl.DeviceIdType.MESH
COLS = (((1,), (1,)), ((), ()))


def shifted(block, axis, distance):
    devices = range(lax.axis_size(axis))
    route = [(i - distance, i) for i in devices if i - distance in devices]
    return lax.ppermute(block, axis, route)


def dot(a, b, dims=(((1,), (0,)), ((), ()))):
    return lax.dot_general(a, b, dims, preferred_element_type=F32)


def summary_kernel(lin_scale, size, q, k, v, g, col, out):
    heads = q.shape[1] // size
    states, grads = [], []
    for j in range(heads):
        cut = slice(j * size, (j + 1) * size)
        run = col[0, :, j : j + 1]
        fading = jnp.exp(run[run.shape[0] - 1 :, :] - run)
        weighted = (v[:, cut].astype(F32) * fading).astype(BF16)
        scaled = (g[:, cut].astype(F32) * jnp.exp(run)).astype(BF16)
        states.append(dot(k[:, cut], weighted, ROWS))
        grads.append(lin_scale * dot(q[:, cut], scaled, ROWS))
    out[:size, :] = jnp.concatenate(states, axis=1).astype(BF16)
    out[size:, :] = jnp.concatenate(grads, axis=1).astype(BF16)


def near_pair(lin_scale, soft_scale, size, q, k, v, g, pk, pv, col, row, times):
    rows = q.shape[0]
    heads = q.shape[1] // size
    t = lax.broadcasted_iota(jnp.int32, (rows, rows), 0)
    s = lax.broadcasted_iota(jnp.int32, (rows, rows), 1)
    lower = t >= s
    outs, dqs, dkv, dvv = [], [], [], []
    for j in range(heads):
        cut = slice(j * size, (j + 1) * size)
        qh, gh = q[:, cut], g[:, cut]
        kh = jnp.concatenate([k[:, cut], pk[:, cut]], axis=0)
        vh = jnp.concatenate([v[:, cut], pv[:, cut]], axis=0)
        decay = jnp.where(
            lower, jnp.exp(jnp.minimum(col[:, j : j + 1] - row[j : j + 1, :], 0.0)), 0.0
        ) * lin_scale
        score = dot(qh, kh, COLS)
        grad = dot(gh, vh, COLS)
        logits = jnp.where(times > 0.0, score * soft_scale, -1e30)
        peak = jnp.max(logits, axis=1, keepdims=True)
        terms = jnp.exp(logits - peak) * times
        probs = terms / jnp.sum(terms, axis=1, keepdims=True)
        inner = jnp.sum(probs * grad, axis=1, keepdims=True)
        dlogit = probs * (grad - inner) * soft_scale
        mix = jnp.concatenate(
            [probs[:, :rows] + score[:, :rows] * decay, probs[:, rows:]], axis=1
        ).astype(BF16)
        dmix = jnp.concatenate(
            [dlogit[:, :rows] + grad[:, :rows] * decay, dlogit[:, rows:]], axis=1
        ).astype(BF16)
        outs.append(dot(mix, vh))
        dqs.append(dot(dmix, kh))
        dkv.append(dot(dmix, qh, ROWS))
        dvv.append(dot(mix, gh, ROWS))
    dk = jnp.concatenate(dkv, axis=1)
    dv = jnp.concatenate(dvv, axis=1)
    return (
        jnp.concatenate(outs, axis=1),
        jnp.concatenate(dqs, axis=1),
        dk[:rows],
        dv[:rows],
        dk[rows:].astype(BF16),
        dv[rows:].astype(BF16),
    )


def state_kernel(
    lin_scale, size, q, k, v, g, col, carry, out, dq, own_k, own_v,
    layer, delta, grad_k, grad_v,
):
    heads = q.shape[1] // size
    state, later = carry[:size, :], carry[size:, :]
    outs, dqs, dks, dvs = [], [], [], []
    for j in range(heads):
        cut = slice(j * size, (j + 1) * size)
        run = col[0, :, j : j + 1]
        growth = lin_scale * jnp.exp(run)
        fading = jnp.exp(run[run.shape[0] - 1 :, :] - run)
        st, lt = state[:, cut], later[:, cut]
        outs.append(growth * dot(q[:, cut], st))
        dqs.append(growth * dot(g[:, cut], st, COLS))
        dks.append(fading * dot(v[:, cut], lt, COLS))
        dvs.append(fading * dot(k[:, cut], lt))
    layer[...] = (out[...] + jnp.concatenate(outs, axis=1)).astype(BF16)
    delta[...] = (dq[...] + jnp.concatenate(dqs, axis=1)).astype(BF16)
    grad_k[...] = (own_k[...] + jnp.concatenate(dks, axis=1)).astype(BF16)
    grad_v[...] = (own_v[...] + jnp.concatenate(dvs, axis=1)).astype(BF16)


def attention_parts(row_count, feat_width, head_count):
    size = feat_width // head_count
    pair = 256 // size
    steps = head_count // pair
    lanes = pair * size
    wide = pl.BlockSpec((row_count, lanes), lambda i: (0, i))
    col = pl.BlockSpec((1, row_count, pair), lambda i: (i, 0, 0))
    row = pl.BlockSpec((1, pair, row_count), lambda i: (i, 0, 0))
    return size, pair, steps, lanes, wide, col, row


def project(inputs, weight):
    return dot(inputs, weight).astype(BF16)


def shards(tokens, query_weight, key_weight, value_weight, log_decay, neighbour_blocks, cotangent):
    row_count, feat_width = tokens.shape
    head_count = log_decay.shape[0]
    size, pair, steps, lanes, wide, col_spec, row_spec = attention_parts(
        row_count, feat_width, head_count
    )
    lin_scale = 1.0 / (size * math.sqrt(row_count))
    soft_scale = 1.0 / math.sqrt(size)
    sizes = tuple(lax.axis_size(name) for name in AXES)
    devices = sizes[0] * sizes[1]
    position = lax.axis_index(AXES)
    shape = lambda dtype: jax.ShapeDtypeStruct((row_count, feat_width), dtype)

    prev_tokens = shifted(tokens, AXES, 1)
    running = jnp.cumsum(log_decay, axis=1)
    row = running.reshape(steps, pair, row_count)
    col = row.transpose(0, 2, 1)
    query = project(tokens, query_weight)
    key = project(tokens, key_weight)
    value = project(tokens, value_weight)

    summary = pl.pallas_call(
        functools.partial(summary_kernel, lin_scale, size),
        grid=(steps,),
        in_specs=[wide] * 4 + [col_spec],
        out_specs=pl.BlockSpec((2 * size, lanes), lambda i: (0, i)),
        out_shape=jax.ShapeDtypeStruct((2 * size, feat_width), BF16),
        cost_estimate=pl.CostEstimate(flops=10**8, bytes_accessed=10**6, transcendentals=0),
    )(query, key, value, cotangent, col)
    total = jnp.broadcast_to(jnp.repeat(running[:, -1], size)[None, :], (8, feat_width))

    prev_key = project(prev_tokens, key_weight)
    prev_value = project(prev_tokens, value_weight)
    own_times = jnp.sum(neighbour_blocks == position).astype(F32)
    prev_times = jnp.sum(neighbour_blocks == position - 1).astype(F32)
    times = jnp.where(jnp.arange(2 * row_count) < row_count, own_times, prev_times)[None, :]
    near = functools.partial(near_pair, lin_scale, soft_scale, size)
    operands = (query, key, value, cotangent, prev_key, prev_value, col, row, times)
    carry, out, dq, own_k, own_v, prev_gk, prev_gv = carried(near, summary, total, operands, sizes)

    owed = dot(prev_gk, key_weight, COLS) + dot(prev_gv, value_weight, COLS)
    owed = shifted(owed.astype(BF16), AXES, -1)

    layer_out, query_delta, grad_k, grad_v = pl.pallas_call(
        functools.partial(state_kernel, lin_scale, size),
        grid=(steps,),
        in_specs=[wide] * 4
        + [col_spec, pl.BlockSpec((2 * size, lanes), lambda i: (0, i))]
        + [wide] * 4,
        out_specs=[wide] * 4,
        out_shape=[shape(BF16)] * 4,
        cost_estimate=pl.CostEstimate(flops=10**9, bytes_accessed=10**7, transcendentals=0),
    )(query, key, value, cotangent, col, carry, out, dq, own_k, own_v)

    grad_norm = 1.0 / math.sqrt(row_count * devices)
    grads = reduce_grads(
        grad_norm,
        (tokens, prev_tokens, query_delta, grad_k, grad_v, prev_gk, prev_gv),
        sizes,
    )
    tokens_back = dot(query_delta, query_weight, COLS)
    tokens_back = tokens_back + dot(grad_k, key_weight, COLS) + dot(grad_v, value_weight, COLS)
    tokens_back = tokens_back + owed.astype(F32)
    return (layer_out, tokens_back.astype(BF16), *grads)


def bits_of(axis, size):
    return [(axis, k) for k in range(size.bit_length() - 1)]


def bit_of(bit):
    return (lax.axis_index(bit[0]) // 2 ** bit[1]) % 2


def partner_of(bit):
    place = {name: lax.axis_index(name) for name in AXES}
    place[bit[0]] = place[bit[0]] + (1 - 2 * bit_of(bit)) * 2 ** bit[1]
    return place


def greet(bits):
    barrier = pltpu.get_barrier_semaphore()
    for bit in bits:
        pl.semaphore_signal(barrier, inc=1, device_id=partner_of(bit), device_id_type=MESH)
    pl.semaphore_wait(barrier, len(bits))


def carry_kernel(bits, near, size, x, total, *refs):
    ins, col, row, count = refs[:6], refs[6], refs[7], refs[8]
    out, results = refs[9], refs[10:16]
    sent, came, sums, sums_came, carry, sem, sum_sem = refs[16:]
    steps, _, pair = col.shape
    lanes = pair * size

    def near_step(i, _):
        cut = pl.ds(pl.multiple_of(i * lanes, lanes), lanes)
        values = near(*(ref[:, cut] for ref in ins), col[i], row[i], count[...])
        for ref, value in zip(results, values):
            ref[:, cut] = value
        return 0

    greet(bits)
    stages = len(bits)
    width = x.shape[1]
    tf = x[:size, :].astype(F32)
    tb = x[size:, :].astype(F32)
    carry[...] = jnp.zeros_like(carry)
    log_all = total[...]
    log_before = jnp.zeros_like(log_all)
    log_after = jnp.zeros_like(log_all)
    for i, bit in enumerate(bits):
        mine = bit_of(bit)
        if i:
            sums[i] = log_all
            sent[i, :size, :] = tf.astype(BF16)
            sent[i, size:, :] = tb.astype(BF16)
        rows = slice(None) if i + 1 < stages else pl.ds(pl.multiple_of(mine * size, size), size)
        copies = [
            pltpu.make_async_remote_copy(
                src_ref=sent.at[i, rows] if i else x.at[rows], dst_ref=came.at[i, rows],
                send_sem=sem.at[0, i], recv_sem=sem.at[1, i],
                device_id=partner_of(bit), device_id_type=MESH,
            ),
            pltpu.make_async_remote_copy(
                src_ref=sums.at[i] if i else total, dst_ref=sums_came.at[i],
                send_sem=sum_sem.at[0, i], recv_sem=sum_sem.at[1, i],
                device_id=partner_of(bit), device_id_type=MESH,
            ),
        ]
        for copy in copies:
            copy.start()
        lax.fori_loop(steps * i // stages, steps * (i + 1) // stages, near_step, 0)
        for copy in copies:
            copy.wait()
        log_other = sums_came[i]
        if i + 1 == stages:
            rows = pl.ds(pl.multiple_of((1 - mine) * size, size), size)
            gap = jnp.where(jnp.full((1, width), mine) == 1, log_before[:1], log_after[:1])
            carry[rows, :] += jnp.exp(gap) * came[i, rows, :].astype(F32)
            break
        f_other = came[i, :size, :].astype(F32)
        b_other = came[i, size:, :].astype(F32)
        second = jnp.full((1, width), mine) == 1
        scale = jnp.exp(jnp.where(second, log_before, log_after)[:1])
        carry[:size, :] += jnp.where(second, scale, 0.0) * f_other
        carry[size:, :] += jnp.where(second, 0.0, scale) * b_other
        log_before = log_before + jnp.where(second, log_other, 0.0)
        log_after = log_after + jnp.where(second, 0.0, log_other)
        here, there = jnp.exp(log_all[:1]), jnp.exp(log_other[:1])
        one = jnp.ones_like(here)
        tf = jnp.where(second, one, there) * tf + jnp.where(second, here, one) * f_other
        tb = jnp.where(second, there, one) * tb + jnp.where(second, one, here) * b_other
        log_all = log_all + log_other
    out[...] = carry[...].astype(BF16)


def carried(near, summary, total, operands, sizes):
    bits = bits_of("span", sizes[1]) + bits_of("group", sizes[0])
    rows, width = summary.shape
    stages = len(bits)
    vmem = pl.BlockSpec(memory_space=pltpu.VMEM)
    return pl.pallas_call(
        functools.partial(carry_kernel, bits, near, rows // 2),
        in_specs=[vmem] * (2 + len(operands)),
        out_specs=[vmem] * 7,
        out_shape=[jax.ShapeDtypeStruct((rows, width), BF16)]
        + [jax.ShapeDtypeStruct(operands[0].shape, F32)] * 4
        + [jax.ShapeDtypeStruct(operands[0].shape, BF16)] * 2,
        scratch_shapes=[
            pltpu.VMEM((stages, rows, width), BF16),
            pltpu.VMEM((stages, rows, width), BF16),
            pltpu.VMEM((stages, 8, width), F32),
            pltpu.VMEM((stages, 8, width), F32),
            pltpu.VMEM((rows, width), F32),
            pltpu.SemaphoreType.DMA((2, stages)),
            pltpu.SemaphoreType.DMA((2, stages)),
        ],
        compiler_params=pltpu.CompilerParams(collective_id=0, has_side_effects=True),
        cost_estimate=pl.CostEstimate(flops=10**9, bytes_accessed=10**8, transcendentals=0),
    )(summary, total, *operands)


def reduce_kernel(orders, norm, tokens, prev, dq, dk, dv, pk, pv, *refs):
    count = len(orders)
    outs = refs[:count]
    made, held, acc, sem = refs[count:]
    parts = [made.at[p] for p in range(count)]
    deltas = ((dq, None), (dk, pk), (dv, pv))
    stages = len(orders[0])
    whole = outs[0].shape[0]
    greet(orders[0])

    def make(p, start):
        own, other = deltas[p]
        right = own[...] if other is None else jnp.concatenate([own[...], other[...]], axis=0)

        def one(c, _):
            cut = pl.ds(pl.multiple_of(start * 8 + c * 128, 128), 128)
            left = tokens[:, cut]
            if other is not None:
                left = jnp.concatenate([left, prev[:, cut]], axis=0)
            block = dot(left, right, ROWS) * norm
            made[p, pl.ds(start + c * 16, 16)] = block.reshape(16, 8, -1).astype(BF16)
            return 0

        lax.fori_loop(0, whole // 32, one, 0)

    low = [[0] for _ in orders]

    def halves(p, i):
        half = whole >> (i + 1)
        mine = bit_of(orders[p][i])
        keep = low[p][i] + mine * half
        give = low[p][i] + (1 - mine) * half
        return half, keep, give

    def copy(src, dst, p, i, slot):
        return pltpu.make_async_remote_copy(
            src_ref=src, dst_ref=dst, send_sem=sem.at[0, p, slot], recv_sem=sem.at[1, p, slot],
            device_id=partner_of(orders[p][i]), device_id_type=MESH,
        )

    def scatter(p, i):
        half, keep, give = halves(p, i)
        source = parts[p] if i == 0 else acc.at[p]
        place = whole - 2 * half
        return copy(source.at[pl.ds(give, half)], held.at[p, pl.ds(place, half)], p, i, i)

    def gather(p, i):
        half, keep, _ = halves(p, i)
        block = outs[p].at[pl.ds(keep, half)]
        return copy(block, block, p, i, stages + i)

    going = []
    for p in range(count):
        make(p, halves(p, 0)[2])
        going.append(scatter(p, 0))
        going[p].start()
    for p in range(count):
        make(p, halves(p, 0)[1])
    for i in range(stages):
        for p in range(count):
            going[p].wait()
            half, keep, _ = halves(p, i)
            source = parts[p] if i == 0 else acc.at[p]
            target = acc.at[p] if i + 1 < stages else outs[p]
            place = whole - 2 * half
            step = min(half, 8)

            def add(c, _):
                at = pl.ds(keep + c * step, step)
                target[at] = source[at] + held[p, pl.ds(place + c * step, step)]
                return 0

            lax.fori_loop(0, half // step, add, 0)
            low[p].append(keep)
            going[p] = scatter(p, i + 1) if i + 1 < stages else gather(p, i)
            going[p].start()
    for i in reversed(range(stages)):
        for p in range(count):
            going[p].wait()
            if i:
                going[p] = gather(p, i - 1)
                going[p].start()


def reduce_grads(norm, operands, sizes):
    group, span = bits_of("group", sizes[0]), bits_of("span", sizes[1])
    rest = group[1:] + span
    turns = [rest[k:3] + rest[:k] + rest[3:] for k in range(3)]
    orders = [group[:1] + turn for turn in turns]
    rows = width = operands[0].shape[1]
    deep = (rows // 8, 8, width)
    vmem = pl.BlockSpec(memory_space=pltpu.VMEM)
    stages = len(orders[0])
    outs = pl.pallas_call(
        functools.partial(reduce_kernel, orders, norm),
        in_specs=[vmem] * len(operands),
        out_specs=[vmem] * 3,
        out_shape=[jax.ShapeDtypeStruct(deep, BF16)] * 3,
        scratch_shapes=[
            pltpu.VMEM((3, *deep), BF16),
            pltpu.VMEM((3, *deep), BF16),
            pltpu.VMEM((3, *deep), BF16),
            pltpu.SemaphoreType.DMA((2, 3, 2 * stages)),
        ],
        compiler_params=pltpu.CompilerParams(
            collective_id=1, has_side_effects=True, vmem_limit_bytes=40 * 2**20
        ),
        cost_estimate=pl.CostEstimate(flops=10**9, bytes_accessed=10**8, transcendentals=0),
    )(*operands)
    return [out.reshape(rows, width) for out in outs]


def solution(mesh):
    return jax.shard_map(
        shards,
        mesh=mesh,
        in_specs=(
            P(AXES, None),
            P(),
            P(),
            P(),
            P(None, AXES),
            P(AXES, None),
            P(AXES, None),
        ),
        out_specs=(P(AXES, None), P(AXES, None), P(), P(), P()),
        check_vma=False,
    )
```
